1024 devices in a mesh: row: 16 (over x, y_lo), col: 64 (over y_hi, z, core).
Axes of the slice: x: 8, y: 8 (y_hi: 4, y_lo: 2; y = y_hi * 2 + y_lo), z: 8, core: 2. Of those that a mesh axis runs over, the one named last changes fastest.
Arguments:
- tokens: bfloat16 [640, 8192], P('col', 'row'), may hold values from -6 to 6
- cotangent: bfloat16 [640, 8192], P('col', 'row'), may hold values from -6 to 6
- gate_tiles: bfloat16 [96, 8192, 128], P('row', 'col'), may hold values from -0.125 to 0.125
- up_tiles: bfloat16 [96, 8192, 128], P('row', 'col'), may hold values from -0.125 to 0.125
- down_tiles: bfloat16 [96, 8192, 128], P('row', 'col'), may hold values from -0.09375 to 0.09375
- tile_index: int32 [3, 96, 128], P(None, 'row', 'col'), may hold values from 0 to 3, as said below
- tile_counts: int32 [3, 16, 64], P(None, 'row', 'col'), may hold values from 1 to 6, as said below
Outputs:
- output: bfloat16 [640, 8192], P('col', 'row')
- input_grad: bfloat16 [640, 8192], P('col', 'row')
- gate_grad: float32 [96, 8192, 128], P('row', 'col')
- up_grad: float32 [96, 8192, 128], P('row', 'col')
- down_grad: float32 [96, 8192, 128], P('row', 'col')
The draws below stay inside these ranges and needn't reach their ends.
Inputs may be any that keep to these rules, and one draw needn't show every extreme that they name: `tile_index`: within one matrix, row group and column group, the 6 slots name distinct block pairs; for gate and up the row block is below 4 and the column block below 2, for down the row block is below 2 and the column block below 4. `tile_counts`: for each matrix some row group and column group has all 6 slots live.
All inputs are finite; a program needn't handle non-finite values.
Results may differ from the reference program's by a relative error of at most 0.0049.
Values may be sent and summed in bfloat16 or wider, within the bound.
No kernel may reach another device: no remote copies, remote signals or barrier semaphores. Data moves between devices by JAX's collectives and lax.ppermute only.
A program may use at most 32 MiB of HBM per device.

```python
import jax
import jax.numpy as jnp

D = 8192
FF = 16384
TB = 128
CAP = 6
ROW_GROUPS = 16
COL_GROUPS = 64
TOKENS = 640
RB = 4
CB = 2
SLOTS = 96
TILE_COLS = 8192


def first_slots(one_key):
    return jax.random.permutation(one_key, RB * CB)[:CAP]


def draw_tile_index(key, part):
    group_total = 3 * ROW_GROUPS * COL_GROUPS
    key_list = jax.random.split(jax.random.fold_in(key, 17), group_total)
    chosen = jax.vmap(first_slots)(key_list).reshape(3, ROW_GROUPS, COL_GROUPS, CAP)
    down_pick = (jnp.arange(3) == 2)[:, None, None, None]
    row_blocks = jnp.where(down_pick, chosen // RB, chosen // CB)
    col_blocks = jnp.where(down_pick, chosen % RB, chosen % CB)
    pair_list = jnp.stack([row_blocks, col_blocks], axis=-1)
    pair_list = pair_list.transpose(0, 1, 3, 2, 4).reshape(3, ROW_GROUPS * CAP, COL_GROUPS * 2)
    return pair_list.astype(jnp.int32)


def draw_tile_counts(key, part):
    key_base, key_heavy, key_forced = jax.random.split(jax.random.fold_in(key, 29), 3)
    grid_shape = (3, ROW_GROUPS, COL_GROUPS)
    base_counts = jax.random.randint(key_base, grid_shape, 1, 4)
    heavy_mask = jax.random.randint(key_heavy, grid_shape, 0, 16) == 0
    counts = jnp.where(heavy_mask, CAP, base_counts).reshape(3, ROW_GROUPS * COL_GROUPS)
    forced = jax.random.randint(key_forced, (3,), 0, ROW_GROUPS * COL_GROUPS)
    counts = counts.at[jnp.arange(3), forced].set(CAP)
    return counts.reshape(grid_shape).astype(jnp.int32)


def steps_of(rng, dims, shards, least, largest):
    loudness, own = 1.0, jax.random.fold_in(rng, 6)
    for position, blocks in shards:
        steps = jnp.exp(jax.random.uniform(jax.random.fold_in(own, position), (blocks,), jnp.float32, least / len(shards), largest / len(shards)))
        loudness = loudness * jnp.repeat(steps, dims[position] // blocks).reshape([-1 if axis == position else 1 for axis in range(len(dims))])
    return loudness


def noise(key, dims, spread, most, cuts=(), kind=jnp.bfloat16):
    entries = spread * jax.random.normal(key, dims, jnp.float32)
    if cuts:
        entries = entries * steps_of(key, dims, cuts, -0.22, 0.18)
    return jnp.clip(entries, -most, most).astype(kind)


def setup_inputs(seed: int = 0) -> dict:
    splits = jax.random.split(jax.random.key(seed), 8)
    tokens = noise(splits[0], (TOKENS, D), 1.0, 6.0, ((0, 64), (1, 16)))
    cotangent = noise(splits[1], (TOKENS, D), 1.0, 6.0, ((0, 64), (1, 16)))
    gate_tiles = noise(splits[2], (SLOTS, TILE_COLS, TB), (D // 4) ** -0.5, 0.125, ((0, 16), (1, 64)))
    up_tiles = noise(splits[3], (SLOTS, TILE_COLS, TB), (D // 4) ** -0.5, 0.125, ((0, 16), (1, 64)))
    down_tiles = noise(splits[4], (SLOTS, TILE_COLS, TB), (FF // 4) ** -0.5, 0.09375, ((0, 16), (1, 64)))
    tile_index = draw_tile_index(jax.random.fold_in(splits[7], 71), 0)
    tile_counts = draw_tile_counts(jax.random.fold_in(splits[7], 71), 0)
    return dict(tokens=tokens, cotangent=cotangent, gate_tiles=gate_tiles, up_tiles=up_tiles, down_tiles=down_tiles, tile_index=tile_index, tile_counts=tile_counts)


def place_tiles(tiles, index, counts, row_count, col_count, is_down):
    tile_size = TB
    slot_count = CAP
    row_groups, col_groups = counts.shape
    blocks = tiles.reshape(row_groups, slot_count, col_groups, tile_size, tile_size).transpose(0, 2, 1, 3, 4)
    pair_list = index.reshape(row_groups, slot_count, col_groups, 2).transpose(0, 2, 1, 3)
    live_mask = jnp.arange(slot_count).astype(jnp.int32)[None, None, :] < counts[:, :, None]
    blocks = jnp.where(live_mask[..., None, None], blocks, jnp.zeros_like(blocks))
    row_group_ids = jnp.arange(row_groups).astype(jnp.int32)[:, None, None]
    col_group_ids = jnp.arange(col_groups).astype(jnp.int32)[None, :, None]
    if is_down:
        grid_rows = (col_group_ids * row_count + pair_list[..., 0]).astype(jnp.int32)
        grid_cols = (row_group_ids * col_count + pair_list[..., 1]).astype(jnp.int32)
        total_rows = col_groups * row_count
        total_cols = row_groups * col_count
    else:
        grid_rows = (row_group_ids * row_count + pair_list[..., 0]).astype(jnp.int32)
        grid_cols = (col_group_ids * col_count + pair_list[..., 1]).astype(jnp.int32)
        total_rows = row_groups * row_count
        total_cols = col_groups * col_count
    grid = jnp.zeros((total_rows, total_cols, tile_size, tile_size), tiles.dtype)
    grid = grid.at[grid_rows, grid_cols].add(blocks)
    dense = grid.transpose(0, 2, 1, 3).reshape(total_rows * tile_size, total_cols * tile_size)
    return dense, grid_rows, grid_cols, live_mask


def extract_tiles(full, grid_rows, grid_cols, live_mask):
    tile_size = TB
    total_rows = full.shape[0] // tile_size
    total_cols = full.shape[1] // tile_size
    grid = full.reshape(total_rows, tile_size, total_cols, tile_size).transpose(0, 2, 1, 3)
    chosen = grid[grid_rows, grid_cols]
    chosen = jnp.where(live_mask[..., None, None], chosen, jnp.zeros_like(chosen))
    row_groups, col_groups, slot_count = live_mask.shape
    return chosen.transpose(0, 2, 1, 3, 4).reshape(row_groups * slot_count, col_groups * tile_size, tile_size)


def reference(tokens, cotangent, gate_tiles, up_tiles, down_tiles, tile_index, tile_counts):
    w_gate, gate_rows, gate_cols, gate_live = place_tiles(gate_tiles, tile_index[0], tile_counts[0], RB, CB, False)
    w_up, up_rows, up_cols, up_live = place_tiles(up_tiles, tile_index[1], tile_counts[1], RB, CB, False)
    w_down, down_rows, down_cols, down_live = place_tiles(down_tiles, tile_index[2], tile_counts[2], CB, RB, True)
    gate_sum = jnp.dot(tokens, w_gate, preferred_element_type=jnp.float32)
    up_sum = jnp.dot(tokens, w_up, preferred_element_type=jnp.float32)
    sigmoid_gate = jax.nn.sigmoid(gate_sum)
    active = gate_sum * sigmoid_gate
    hidden = (active * up_sum).astype(jnp.bfloat16)
    output = jnp.dot(hidden, w_down, preferred_element_type=jnp.float32).astype(jnp.bfloat16)
    hidden_grad = jnp.dot(cotangent, w_down.T, preferred_element_type=jnp.float32)
    gate_act = (hidden_grad * up_sum * sigmoid_gate * (1.0 + gate_sum * (1.0 - sigmoid_gate))).astype(jnp.bfloat16)
    up_act = (hidden_grad * active).astype(jnp.bfloat16)
    input_sum = jnp.dot(gate_act, w_gate.T, preferred_element_type=jnp.float32) + jnp.dot(up_act, w_up.T, preferred_element_type=jnp.float32)
    input_grad = input_sum.astype(jnp.bfloat16)
    gate_grad = extract_tiles(jnp.dot(tokens.T, gate_act, preferred_element_type=jnp.float32), gate_rows, gate_cols, gate_live)
    up_grad = extract_tiles(jnp.dot(tokens.T, up_act, preferred_element_type=jnp.float32), up_rows, up_cols, up_live)
    down_grad = extract_tiles(jnp.dot(hidden.T, cotangent, preferred_element_type=jnp.float32), down_rows, down_cols, down_live)
    return (output, input_grad, gate_grad, up_grad, down_grad)
```

```python
import jax
import jax.numpy as jnp
from jax import lax
from jax.experimental import pallas as pl
from jax.experimental.pallas import tpu as pltpu
from jax.sharding import Mesh
from jax.sharding import PartitionSpec as P

F32 = jnp.float32
BF16 = jnp.bfloat16
VMEM = pl.BlockSpec(memory_space=pltpu.VMEM)
SMEM = pl.BlockSpec(memory_space=pltpu.SMEM)
NT = (((1,), (1,)), ((), ()))
TN = (((0,), (0,)), ((), ()))


def dot(left, right, dims=None):
    if dims is None:
        return jnp.dot(left, right, preferred_element_type=F32)
    return lax.dot_general(left, right, dims, preferred_element_type=F32)


def fill_weight(dense, tiles, index, counts, which):
    dense[...] = jnp.zeros_like(dense)
    side = tiles.shape[-1]
    for slot in range(tiles.shape[0]):

        @pl.when(slot < counts[which])
        def _():
            rows = pl.ds(pl.multiple_of(index[which, slot, 0] * side, side), side)
            cols = pl.ds(pl.multiple_of(index[which, slot, 1] * side, side), side)
            dense[rows, cols] = tiles[slot]


def take_tiles(out, dense, index, counts, which, col_offset=0):
    side = out.shape[-1]
    for slot in range(out.shape[0]):
        live = slot < counts[which]

        @pl.when(live)
        def _():
            rows = pl.ds(pl.multiple_of(index[which, slot, 0] * side, side), side)
            cols = pl.ds(
                pl.multiple_of(index[which, slot, 1] * side + col_offset, side), side
            )
            out[slot] = dense[rows, cols]

        @pl.when(jnp.logical_not(live))
        def _():
            out[slot] = jnp.zeros(out.shape[1:], out.dtype)


def spread_kernel(tokens, cotangent, out, stage):
    rows, lanes = tokens.shape
    side = out.shape[-1]
    for q in range(lanes // side):
        cols = slice(q * side, (q + 1) * side)
        stage[(2 * q) * rows : (2 * q + 1) * rows, :] = tokens[:, cols].astype(F32)
        stage[(2 * q + 1) * rows : (2 * q + 2) * rows, :] = cotangent[:, cols].astype(F32)
    block = stage[...].astype(out.dtype)
    for peer in range(out.shape[0]):
        out[peer] = block


def partial_kernel(
    index, counts, own_t, own_c, far_t, far_c, gate, up, down, out, w_gate, w_up, w_down
):
    fill_weight(w_gate, gate, index, counts, 0)
    fill_weight(w_up, up, index, counts, 1)
    fill_weight(w_down, down, index, counts, 2)
    half = own_t.shape[0]
    units = w_gate.shape[1]
    for start, toks, cots in ((0, own_t, own_c), (half, far_t, far_c)):
        rows = slice(start, start + half)
        out[rows, 0:units] = dot(toks[...], w_gate[...]).astype(out.dtype)
        out[rows, units : 2 * units] = dot(toks[...], w_up[...]).astype(out.dtype)
        out[rows, 2 * units :] = dot(cots[...], w_down[...], NT).astype(out.dtype)


def units_kernel(parts, out):
    total = parts[0].astype(F32)
    for peer in range(1, parts.shape[0]):
        total = total + parts[peer].astype(F32)
    units = total.shape[1] // 3
    gate_sum = total[:, 0:units]
    up_sum = total[:, units : 2 * units]
    hidden_grad = total[:, 2 * units :]
    sigmoid_gate = jax.nn.sigmoid(gate_sum)
    active = gate_sum * sigmoid_gate
    hidden = (active * up_sum).astype(out.dtype)
    gate_act = (
        hidden_grad * up_sum * sigmoid_gate * (1.0 + gate_sum * (1.0 - sigmoid_gate))
    ).astype(out.dtype)
    up_act = (hidden_grad * active).astype(out.dtype)
    for peer in range(out.shape[0]):
        out[peer, :, 0:units] = hidden
        out[peer, :, units : 2 * units] = gate_act
        out[peer, :, 2 * units :] = up_act


def apply_back(acts, rows, w_gate, w_up, w_down, out):
    units = w_gate.shape[1]
    lanes = w_gate.shape[0]
    out[:, 0:lanes] = dot(acts[rows, 0:units], w_down[...]).astype(out.dtype)
    out[:, lanes:] = (
        dot(acts[rows, units : 2 * units], w_gate[...], NT)
        + dot(acts[rows, 2 * units :], w_up[...], NT)
    ).astype(out.dtype)


def far_kernel(index, counts, acts, gate, up, down, out, w_gate, w_up, w_down):
    fill_weight(w_gate, gate, index, counts, 0)
    fill_weight(w_up, up, index, counts, 1)
    fill_weight(w_down, down, index, counts, 2)
    half = out.shape[0]
    apply_back(acts, slice(half, 2 * half), w_gate, w_up, w_down, out)


def own_kernel(index, counts, acts, gate, up, down, out, w_gate, w_up, w_down):
    fill_weight(w_gate, gate, index, counts, 0)
    fill_weight(w_up, up, index, counts, 1)
    fill_weight(w_down, down, index, counts, 2)
    apply_back(acts, slice(0, out.shape[0]), w_gate, w_up, w_down, out)


def grads_kernel(
    index, counts, acts, own_t, own_c, far_t, far_c, gate_out, up_out, down_out, dense, dense_down
):
    half = own_t.shape[0]
    units = dense_down.shape[0]
    dense[...] = dot(own_t[...], acts[0:half, units:], TN) + dot(far_t[...], acts[half:, units:], TN)
    dense_down[...] = dot(acts[0:half, 0:units], own_c[...], TN) + dot(
        acts[half:, 0:units], far_c[...], TN
    )
    take_tiles(gate_out, dense, index, counts, 0)
    take_tiles(up_out, dense, index, counts, 1, units)
    take_tiles(down_out, dense_down, index, counts, 2)


def finish_kernel(parts, output, input_grad):
    total = parts[0].astype(F32)
    for peer in range(1, parts.shape[0]):
        total = total + parts[peer].astype(F32)
    rows = output.shape[0]
    side = total.shape[1]
    chunks = output.shape[1] // side
    for q in range(chunks):
        cols = slice(q * side, (q + 1) * side)
        output[:, cols] = total[q * rows : (q + 1) * rows].astype(output.dtype)
        input_grad[:, cols] = total[(chunks + q) * rows : (chunks + q + 1) * rows].astype(
            input_grad.dtype
        )


def call(kernel, outs, specs, *args, scratch=(), flops=0):
    moved = sum(a.size * a.dtype.itemsize for a in args) + sum(
        o.size * jnp.dtype(o.dtype).itemsize for o in outs
    )
    return pl.pallas_call(
        kernel,
        out_shape=outs if len(outs) > 1 else outs[0],
        in_specs=specs,
        out_specs=(VMEM,) * len(outs) if len(outs) > 1 else VMEM,
        scratch_shapes=scratch,
        cost_estimate=pl.CostEstimate(flops=flops, bytes_accessed=moved, transcendentals=0),
    )(*args)


def body(tokens, cotangent, gate_tiles, up_tiles, down_tiles, tile_index, tile_counts):
    rows, lanes = tokens.shape
    slots, side, _ = gate_tiles.shape
    row_size = lax.axis_size("row")
    peers = lax.axis_size("yz")
    units = 2 * side
    chunks = lanes // side
    half = peers * rows
    share = 2 * half // row_size
    counts = tile_counts.reshape(3)
    shape = jax.ShapeDtypeStruct
    weights = (
        pltpu.VMEM((lanes, units), BF16),
        pltpu.VMEM((lanes, units), BF16),
        pltpu.VMEM((units, lanes), BF16),
    )
    swap = [(0, 1), (1, 0)]

    spread = call(
        spread_kernel,
        (shape((peers, 2 * chunks * rows, side), BF16),),
        (VMEM, VMEM),
        tokens,
        cotangent,
        scratch=(pltpu.VMEM((2 * chunks * rows, side), F32),),
    )
    own = lax.all_to_all(spread, "yz", split_axis=0, concat_axis=0, tiled=True)
    far = lax.ppermute(own, "core", swap)

    def unpack(blocks):
        split = blocks.reshape(peers, chunks, 2, rows, side).transpose(2, 0, 3, 1, 4)
        split = split.reshape(2, half, lanes)
        return split[0], split[1]

    own_t, own_c = unpack(own)
    far_t, far_c = unpack(far)
    parts = call(
        partial_kernel,
        (shape((2 * half, 3 * units), BF16),),
        (SMEM, SMEM) + (VMEM,) * 7,
        tile_index,
        counts,
        own_t,
        own_c,
        far_t,
        far_c,
        gate_tiles,
        up_tiles,
        down_tiles,
        scratch=weights,
        flops=12 * half * lanes * units,
    )
    parts = parts.reshape(row_size, share, 3 * units)
    parts = lax.all_to_all(parts, "row", split_axis=0, concat_axis=0, tiled=True)
    acts = call(units_kernel, (shape(parts.shape, BF16),), (VMEM,), parts)
    acts = lax.all_to_all(acts, "row", split_axis=0, concat_axis=0, tiled=True)
    acts = acts.reshape(2 * half, 3 * units)

    weight_args = (tile_index, counts, acts, gate_tiles, up_tiles, down_tiles)
    weight_specs = (SMEM, SMEM) + (VMEM,) * 4
    far_part = call(
        far_kernel,
        (shape((half, 2 * lanes), BF16),),
        weight_specs,
        *weight_args,
        scratch=weights,
        flops=6 * half * lanes * units,
    )
    far_part = lax.ppermute(far_part, "core", swap)
    own_part = call(
        own_kernel,
        (shape((half, 2 * lanes), F32),),
        weight_specs,
        *weight_args,
        scratch=weights,
        flops=6 * half * lanes * units,
    )
    tile_shape = shape((slots, side, side), F32)
    gate_grad, up_grad, down_grad = call(
        grads_kernel,
        (tile_shape,) * 3,
        (SMEM, SMEM) + (VMEM,) * 5,
        tile_index,
        counts,
        acts,
        own_t,
        own_c,
        far_t,
        far_c,
        scratch=(pltpu.VMEM((lanes, 2 * units), F32), pltpu.VMEM((units, lanes), F32)),
        flops=12 * half * lanes * units,
    )
    both = own_part + far_part.astype(F32)
    both = both.reshape(peers, rows, 2 * chunks, side).transpose(0, 2, 1, 3)
    both = both.reshape(peers, 2 * chunks * rows, side).astype(BF16)
    both = lax.all_to_all(both, "yz", split_axis=0, concat_axis=0, tiled=True)
    output, input_grad = call(
        finish_kernel,
        (shape((rows, lanes), BF16),) * 2,
        (VMEM,),
        both,
    )
    return (output, input_grad, gate_grad, up_grad, down_grad)


def solution(mesh):
    row_size, col_size = mesh.shape["row"], mesh.shape["col"]
    split = Mesh(
        mesh.devices.reshape(row_size, col_size // 2, 2), ("row", "yz", "core")
    )
    col = ("yz", "core")
    blocks = P(col, "row")
    tiles = P("row", col, None)
    small = P(None, "row", col)
    return jax.shard_map(
        body,
        mesh=split,
        in_specs=(blocks, blocks, tiles, tiles, tiles, small, small),
        out_specs=(blocks, blocks, tiles, tiles, tiles),
        check_vma=False,
    )
```

```python
import jax
import jax.numpy as jnp
from jax import lax
from jax.experimental import pallas as pl
from jax.experimental.pallas import tpu as pltpu
from jax.sharding import Mesh
from jax.sharding import PartitionSpec as P

F32 = jnp.float32
BF16 = jnp.bfloat16
VMEM = pl.BlockSpec(memory_space=pltpu.VMEM)
SMEM = pl.BlockSpec(memory_space=pltpu.SMEM)
NT = (((1,), (1,)), ((), ()))
TN = (((0,), (0,)), ((), ()))


def dot(left, right, dims=None):
    if dims is None:
        return jnp.dot(left, right, preferred_element_type=F32)
    return lax.dot_general(left, right, dims, preferred_element_type=F32)


def place_tiles(dense, tiles, index, counts, which, row_offset, col_offset):
    side = tiles.shape[-1]
    for slot in range(tiles.shape[0]):

        @pl.when(slot < counts[which])
        def _():
            row = pl.multiple_of(index[which, slot, 0] * side + row_offset, side)
            col = pl.multiple_of(index[which, slot, 1] * side + col_offset, side)
            dense[pl.ds(row, side), pl.ds(col, side)] = tiles[slot]


def weights_kernel(index, counts, gate, up, down, dense):
    lanes = dense.shape[1]
    dense[...] = jnp.zeros_like(dense)
    place_tiles(dense, gate, index, counts, 0, 0, 0)
    place_tiles(dense, up, index, counts, 1, 0, lanes // 2)
    place_tiles(dense, down, index, counts, 2, lanes, 0)


def take_tiles(out, own, far, index, counts, which, row_offset, col_offset):
    side = out.shape[-1]
    for slot in range(out.shape[0]):
        live = slot < counts[which]

        @pl.when(live)
        def _():
            row = pl.multiple_of(index[which, slot, 0] * side + row_offset, side)
            col = pl.multiple_of(index[which, slot, 1] * side + col_offset, side)
            place = (pl.ds(row, side), pl.ds(col, side))
            out[slot] = own[place] + far[place].astype(out.dtype)

        @pl.when(jnp.logical_not(live))
        def _():
            out[slot] = jnp.zeros(out.shape[1:], out.dtype)


def tiles_kernel(index, counts, own, far, gate_out, up_out, down_out):
    lanes = own.shape[1]
    take_tiles(gate_out, own, far, index, counts, 0, 0, 0)
    take_tiles(up_out, own, far, index, counts, 1, 0, lanes // 2)
    take_tiles(down_out, own, far, index, counts, 2, lanes, 0)


def spread_kernel(tokens, cotangent, out, stage):
    rows, lanes = tokens.shape
    side = out.shape[-1]
    chunks = lanes // side
    for start, block in ((0, tokens), (chunks, cotangent)):
        for q in range(chunks):
            piece = block[:, q * side : (q + 1) * side].astype(F32)
            stage[(start + q) * rows : (start + q + 1) * rows, :] = piece
    packed = stage[...].astype(out.dtype)
    for peer in range(out.shape[0]):
        out[peer] = packed


def partial_kernel(blocks, own, far, out, tokens, cotangent, stage):
    peers = blocks.shape[0]
    half, lanes = tokens.shape
    side = blocks.shape[-1]
    rows = half // peers
    chunks = lanes // side
    for peer in range(peers):
        block = blocks[peer].astype(F32)
        for q in range(2 * chunks):
            stage[peer * rows : (peer + 1) * rows, q * side : (q + 1) * side] = block[
                q * rows : (q + 1) * rows
            ]
    tokens[...] = stage[:, 0:lanes].astype(tokens.dtype)
    cotangent[...] = stage[:, lanes:].astype(cotangent.dtype)
    for start, weights in ((0, own), (half, far)):
        out[start : start + half, 0:lanes] = dot(tokens[...], weights[0:lanes, :]).astype(out.dtype)
        out[start : start + half, lanes:] = dot(cotangent[...], weights[lanes:, :], NT).astype(
            out.dtype
        )


def sum_parts(parts):
    total = parts[0].astype(F32)
    for peer in range(1, parts.shape[0]):
        total = total + parts[peer].astype(F32)
    return total


def units_kernel(parts, out):
    total = sum_parts(parts)
    units = total.shape[1] // 3
    gate_sum = total[:, 0:units]
    up_sum = total[:, units : 2 * units]
    hidden_grad = total[:, 2 * units :]
    sigmoid_gate = jax.nn.sigmoid(gate_sum)
    active = gate_sum * sigmoid_gate
    hidden = (active * up_sum).astype(out.dtype)
    gate_act = (
        hidden_grad * up_sum * sigmoid_gate * (1.0 + gate_sum * (1.0 - sigmoid_gate))
    ).astype(out.dtype)
    up_act = (hidden_grad * active).astype(out.dtype)
    for peer in range(out.shape[0]):
        out[peer, :, 0:units] = hidden
        out[peer, :, units : 2 * units] = gate_act
        out[peer, :, 2 * units :] = up_act


def apply_kernel(acts, own, far, out, result, stage):
    half = result.shape[0]
    lanes = own.shape[1]
    units = own.shape[0] - lanes
    peers = out.shape[0]
    side = out.shape[-1]
    rows = half // peers
    near, other = slice(0, half), slice(half, 2 * half)
    result[:, 0:lanes] = dot(acts[near, 0:units], own[lanes:, :]) + dot(
        acts[other, 0:units], far[lanes:, :]
    )
    result[:, lanes:] = dot(acts[near, units:], own[0:lanes, :], NT) + dot(
        acts[other, units:], far[0:lanes, :], NT
    )
    for peer in range(peers):
        for q in range(2 * lanes // side):
            stage[peer, q * rows : (q + 1) * rows, :] = result[
                peer * rows : (peer + 1) * rows, q * side : (q + 1) * side
            ]
        out[peer] = stage[peer].astype(out.dtype)


def grads_kernel(acts, tokens, cotangent, own, far):
    half, lanes = tokens.shape
    units = own.shape[0] - lanes
    for start, out in ((half, far), (0, own)):
        rows = slice(start, start + half)
        out[0:lanes, :] = dot(tokens[...], acts[rows, units:], TN).astype(out.dtype)
        out[lanes:, :] = dot(acts[rows, 0:units], cotangent[...], TN).astype(out.dtype)


def finish_kernel(parts, output, input_grad):
    total = sum_parts(parts)
    rows, lanes = output.shape
    side = total.shape[1]
    chunks = lanes // side
    for start, out in ((0, output), (chunks, input_grad)):
        for q in range(chunks):
            piece = total[(start + q) * rows : (start + q + 1) * rows]
            out[:, q * side : (q + 1) * side] = piece.astype(out.dtype)


def call(kernel, outs, args, smem=0, scratch=(), flops=0):
    moved = sum(a.size * a.dtype.itemsize for a in args) + sum(
        o.size * jnp.dtype(o.dtype).itemsize for o in outs
    )
    single = len(outs) == 1
    return pl.pallas_call(
        kernel,
        out_shape=outs[0] if single else outs,
        in_specs=(SMEM,) * smem + (VMEM,) * (len(args) - smem),
        out_specs=VMEM if single else (VMEM,) * len(outs),
        scratch_shapes=scratch,
        compiler_params=pltpu.CompilerParams(vmem_limit_bytes=20 << 20),
        cost_estimate=pl.CostEstimate(flops=flops, bytes_accessed=moved, transcendentals=0),
    )(*args)


def exchange(blocks, axis):
    return lax.all_to_all(blocks, axis, split_axis=0, concat_axis=0, tiled=True)


def swap(block):
    return lax.ppermute(block, "core", [(0, 1), (1, 0)])


def body(tokens, cotangent, gate_tiles, up_tiles, down_tiles, tile_index, tile_counts):
    rows, lanes = tokens.shape
    slots, side, _ = gate_tiles.shape
    row_size = lax.axis_size("row")
    peers = lax.axis_size("yz")
    units = 2 * side
    half = peers * rows
    share = 2 * half // row_size
    packed = 2 * lanes // side * rows
    flops = 12 * half * lanes * units
    counts = tile_counts.reshape(3)
    shape = jax.ShapeDtypeStruct

    spread = call(
        spread_kernel,
        (shape((peers, packed, side), BF16),),
        (tokens, cotangent),
        scratch=(pltpu.VMEM((packed, side), F32),),
    )
    blocks = exchange(spread, "yz")
    own = call(
        weights_kernel,
        (shape((lanes + units, lanes), BF16),),
        (tile_index, counts, gate_tiles, up_tiles, down_tiles),
        smem=2,
    )
    far = swap(own)
    parts, all_tokens, all_cotangent = call(
        partial_kernel,
        (
            shape((2 * half, 3 * units), BF16),
            shape((half, lanes), BF16),
            shape((half, lanes), BF16),
        ),
        (blocks, own, far),
        scratch=(pltpu.VMEM((half, 2 * lanes), F32),),
        flops=flops,
    )
    parts = exchange(parts.reshape(row_size, share, 3 * units), "row")
    acts = call(units_kernel, (shape(parts.shape, BF16),), (parts,))
    acts = exchange(acts, "row").reshape(2 * half, 3 * units)
    sums = call(
        apply_kernel,
        (shape((peers, packed, side), BF16),),
        (acts, own, far),
        scratch=(pltpu.VMEM((half, 2 * lanes), F32), pltpu.VMEM((peers, packed, side), F32)),
        flops=flops,
    )
    acts, sums = lax.optimization_barrier((acts, sums))
    sums = exchange(sums, "yz")
    own_grad, far_grad = call(
        grads_kernel,
        (shape((lanes + units, lanes), F32), shape((lanes + units, lanes), BF16)),
        (acts, all_tokens, all_cotangent),
        flops=flops,
    )
    gate_grad, up_grad, down_grad = call(
        tiles_kernel,
        (shape((slots, side, side), F32),) * 3,
        (tile_index, counts, own_grad, swap(far_grad)),
        smem=2,
    )
    sums, gate_grad, up_grad, down_grad = lax.optimization_barrier(
        (sums, gate_grad, up_grad, down_grad)
    )
    output, input_grad = call(finish_kernel, (shape((rows, lanes), BF16),) * 2, (sums,))
    return (output, input_grad, gate_grad, up_grad, down_grad)


def solution(mesh):
    row_size, col_size = mesh.shape["row"], mesh.shape["col"]
    split = Mesh(
        mesh.devices.reshape(row_size, col_size // 2, 2), ("row", "yz", "core")
    )
    col = ("yz", "core")
    blocks = P(col, "row")
    tiles = P("row", col, None)
    small = P(None, "row", col)
    return jax.shard_map(
        body,
        mesh=split,
        in_specs=(blocks, blocks, tiles, tiles, tiles, small, small),
        out_specs=(blocks, blocks, tiles, tiles, tiles),
        check_vma=False,
    )
```

```python
import jax
import jax.numpy as jnp
from jax import lax
from jax.experimental import pallas as pl
from jax.experimental.pallas import tpu as pltpu
from jax.sharding import Mesh
from jax.sharding import PartitionSpec as P

F32 = jnp.float32
BF16 = jnp.bfloat16
VMEM = pl.BlockSpec(memory_space=pltpu.VMEM)
SMEM = pl.BlockSpec(memory_space=pltpu.SMEM)
NT = (((1,), (1,)), ((), ()))
TN = (((0,), (0,)), ((), ()))


def dot(left, right, dims=None):
    if dims is None:
        return jnp.dot(left, right, preferred_element_type=F32)
    return lax.dot_general(left, right, dims, preferred_element_type=F32)


def place_tiles(dense, tiles, index, counts, which, row_offset, col_offset):
    side = tiles.shape[-1]
    for slot in range(tiles.shape[0]):

        @pl.when(slot < counts[which])
        def _():
            row = pl.multiple_of(index[which, slot, 0] * side + row_offset, side)
            col = pl.multiple_of(index[which, slot, 1] * side + col_offset, side)
            dense[pl.ds(row, side), pl.ds(col, side)] = tiles[slot]


def weights_kernel(index, counts, gate, up, down, dense):
    lanes = dense.shape[1]
    dense[...] = jnp.zeros_like(dense)
    place_tiles(dense, gate, index, counts, 0, 0, 0)
    place_tiles(dense, up, index, counts, 1, 0, lanes // 2)
    place_tiles(dense, down, index, counts, 2, lanes, 0)


def take_tiles(outs, index, counts, read):
    for which, out in enumerate(outs):
        slots, side, _ = out.shape
        for slot in range(slots):
            live = slot < counts[which]

            @pl.when(live)
            def _():
                row = pl.multiple_of(index[which, slot, 0] * side, side)
                col = pl.multiple_of(index[which, slot, 1] * side, side)
                out[slot] = read(which, slot, row, col)

            @pl.when(jnp.logical_not(live))
            def _():
                out[slot] = jnp.zeros(out.shape[1:], out.dtype)


def place(which, row, col, lanes, side):
    row = pl.multiple_of(row + (lanes if which == 2 else 0), side)
    col = pl.multiple_of(col + (lanes // 2 if which == 1 else 0), side)
    return pl.ds(row, side), pl.ds(col, side)


def pair_kernel(far_index, far_counts, mine, received, own, gate_out, up_out, down_out):
    _, _, lanes = mine.shape
    own[...] = mine[0] + received[0].astype(F32)

    def read(which, slot, row, col):
        at = place(which, row, col, lanes, gate_out.shape[-1])
        return (mine[(1, *at)] + received[(1, *at)].astype(F32)).astype(gate_out.dtype)

    take_tiles((gate_out, up_out, down_out), far_index, far_counts, read)


def tiles_kernel(index, counts, own, gate_far, up_far, down_far, gate_out, up_out, down_out):
    lanes = own.shape[1]
    far = (gate_far, up_far, down_far)

    def read(which, slot, row, col):
        at = place(which, row, col, lanes, gate_out.shape[-1])
        return own[at] + far[which][slot].astype(F32)

    take_tiles((gate_out, up_out, down_out), index, counts, read)


def spread_kernel(tokens, cotangent, out, stage):
    rows, lanes = tokens.shape
    side = out.shape[-1]
    chunks = lanes // side
    part = rows // 2
    peers = out.shape[0] // 2
    size = 2 * chunks * part
    for start, block in ((0, tokens), (chunks, cotangent)):
        for q in range(chunks):
            piece = block[:, q * side : (q + 1) * side].astype(F32)
            for group in range(2):
                row = group * size + (start + q) * part
                stage[row : row + part, :] = piece[group * part : (group + 1) * part]
    for group in range(2):
        packed = stage[group * size : (group + 1) * size, :].astype(out.dtype)
        for peer in range(peers):
            out[group * peers + peer] = packed


def partial_kernel(
    me, blocks, own, far, own_core, far_core, out, tokens, cotangent, stage
):
    _, quarter, lanes = tokens.shape
    side = blocks.shape[-1]
    peers = blocks.shape[0] // 2
    rows = quarter // peers
    chunks = lanes // side
    for group in range(2):
        base = (me[0] if group == 0 else 1 - me[0]) * peers
        for peer in range(peers):
            block = blocks[base + peer].astype(F32)
            for q in range(2 * chunks):
                stage[group, peer * rows : (peer + 1) * rows, q * side : (q + 1) * side] = block[
                    q * rows : (q + 1) * rows
                ]
        tokens[group] = stage[group, :, 0:lanes].astype(tokens.dtype)
        cotangent[group] = stage[group, :, lanes:].astype(cotangent.dtype)
    for start, near, other in ((0, own, far), (quarter, own_core, far_core)):
        rows_out = slice(start, start + quarter)
        out[rows_out, 0:lanes] = (
            dot(tokens[0], near[0:lanes, :]) + dot(tokens[1], other[0:lanes, :])
        ).astype(out.dtype)
        out[rows_out, lanes:] = (
            dot(cotangent[0], near[lanes:, :], NT) + dot(cotangent[1], other[lanes:, :], NT)
        ).astype(out.dtype)


def sum_parts(parts, start, stop):
    total = parts[start].astype(F32)
    for peer in range(start + 1, stop):
        total = total + parts[peer].astype(F32)
    return total


def units_kernel(parts, out):
    total = sum_parts(parts, 0, parts.shape[0])
    units = total.shape[1] // 3
    gate_sum = total[:, 0:units]
    up_sum = total[:, units : 2 * units]
    hidden_grad = total[:, 2 * units :]
    sigmoid_gate = jax.nn.sigmoid(gate_sum)
    active = gate_sum * sigmoid_gate
    hidden = (active * up_sum).astype(out.dtype)
    gate_act = (
        hidden_grad * up_sum * sigmoid_gate * (1.0 + gate_sum * (1.0 - sigmoid_gate))
    ).astype(out.dtype)
    up_act = (hidden_grad * active).astype(out.dtype)
    for peer in range(out.shape[0]):
        out[peer, :, 0:units] = hidden
        out[peer, :, units : 2 * units] = gate_act
        out[peer, :, 2 * units :] = up_act


def apply_kernel(me, acts, own, far, own_core, far_core, out, result, stage):
    quarter = result.shape[0]
    lanes = own.shape[1]
    units = own.shape[0] - lanes
    peers = out.shape[0] // 2
    side = out.shape[-1]
    rows = quarter // peers
    near, other = slice(0, quarter), slice(quarter, 2 * quarter)
    for group, first, second in ((0, own, own_core), (1, far, far_core)):
        result[:, 0:lanes] = dot(acts[near, 0:units], first[lanes:, :]) + dot(
            acts[other, 0:units], second[lanes:, :]
        )
        result[:, lanes:] = dot(acts[near, units:], first[0:lanes, :], NT) + dot(
            acts[other, units:], second[0:lanes, :], NT
        )
        base = (me[0] if group == 0 else 1 - me[0]) * peers
        for peer in range(peers):
            for q in range(2 * lanes // side):
                stage[peer, q * rows : (q + 1) * rows, :] = result[
                    peer * rows : (peer + 1) * rows, q * side : (q + 1) * side
                ]
            out[base + peer] = stage[peer].astype(out.dtype)


def grads_kernel(acts, tokens, cotangent, mine, sibling):
    _, quarter, lanes = tokens.shape
    units = mine.shape[1] - lanes
    for start, out in ((quarter, sibling), (0, mine)):
        rows = slice(start, start + quarter)
        for group in range(2):
            out[group, 0:lanes, :] = dot(tokens[group], acts[rows, units:], TN).astype(out.dtype)
            out[group, lanes:, :] = dot(acts[rows, 0:units], cotangent[group], TN).astype(out.dtype)


def finish_kernel(parts, output, input_grad):
    rows, lanes = output.shape
    part = rows // 2
    peers = parts.shape[0] // 2
    side = parts.shape[-1]
    chunks = lanes // side
    for group in range(2):
        total = sum_parts(parts, group * peers, (group + 1) * peers)
        for start, out in ((0, output), (chunks, input_grad)):
            for q in range(chunks):
                piece = total[(start + q) * part : (start + q + 1) * part]
                out[group * part : (group + 1) * part, q * side : (q + 1) * side] = piece.astype(
                    out.dtype
                )


def call(kernel, outs, args, smem=0, scratch=(), flops=0):
    moved = sum(a.size * a.dtype.itemsize for a in args) + sum(
        o.size * jnp.dtype(o.dtype).itemsize for o in outs
    )
    single = len(outs) == 1
    return pl.pallas_call(
        kernel,
        out_shape=outs[0] if single else outs,
        in_specs=(SMEM,) * smem + (VMEM,) * (len(args) - smem),
        out_specs=VMEM if single else (VMEM,) * len(outs),
        scratch_shapes=scratch,
        compiler_params=pltpu.CompilerParams(vmem_limit_bytes=20 << 20),
        cost_estimate=pl.CostEstimate(flops=flops, bytes_accessed=moved, transcendentals=0),
    )(*args)


def exchange(blocks, axis):
    return lax.all_to_all(blocks, axis, split_axis=0, concat_axis=0, tiled=True)


def swap(block, axis):
    return lax.ppermute(block, axis, [(0, 1), (1, 0)])


def body(tokens, cotangent, gate_tiles, up_tiles, down_tiles, tile_index, tile_counts):
    rows, lanes = tokens.shape
    slots, side, _ = gate_tiles.shape
    row_peers = lax.axis_size("xh") * lax.axis_size("yl")
    peers = lax.axis_size("yz")
    units = 2 * side
    quarter = peers * rows // 2
    share = 2 * quarter // row_peers
    packed = lanes // side * rows
    flops = 24 * quarter * lanes * units
    counts = tile_counts.reshape(3)
    me = lax.axis_index("xl").astype(jnp.int32).reshape(1)
    shape = jax.ShapeDtypeStruct

    spread = call(
        spread_kernel,
        (shape((2 * peers, packed, side), BF16),),
        (tokens, cotangent),
        scratch=(pltpu.VMEM((2 * packed, side), F32),),
    )
    spread, gate_tiles, up_tiles, down_tiles = lax.optimization_barrier(
        (spread, gate_tiles, up_tiles, down_tiles)
    )
    blocks = exchange(spread, ("xl", "yz"))
    own = call(
        weights_kernel,
        (shape((lanes + units, lanes), BF16),),
        (tile_index, counts, gate_tiles, up_tiles, down_tiles),
        smem=2,
    )
    far = swap(own, "xl")
    own_core = swap(own, "core")
    far_core = swap(far, "core")
    listing = jnp.concatenate([tile_index.reshape(3, 2 * slots), counts[:, None]], axis=1)
    listing = swap(listing, "xl")
    far_core, listing = lax.optimization_barrier((far_core, listing))
    far_index = listing[:, 0 : 2 * slots].reshape(3, slots, 2)
    far_counts = listing[:, 2 * slots]
    weights = (own, far, own_core, far_core)
    parts, all_tokens, all_cotangent = call(
        partial_kernel,
        (
            shape((2 * quarter, 3 * units), BF16),
            shape((2, quarter, lanes), BF16),
            shape((2, quarter, lanes), BF16),
        ),
        (me, blocks, *weights),
        smem=1,
        scratch=(pltpu.VMEM((2, quarter, 2 * lanes), F32),),
        flops=flops,
    )
    parts = exchange(parts.reshape(row_peers, share, 3 * units), ("xh", "yl"))
    acts = call(units_kernel, (shape(parts.shape, BF16),), (parts,))
    acts = exchange(acts, ("xh", "yl")).reshape(2 * quarter, 3 * units)
    sums = call(
        apply_kernel,
        (shape((2 * peers, packed, side), BF16),),
        (me, acts, *weights),
        smem=1,
        scratch=(pltpu.VMEM((quarter, 2 * lanes), F32), pltpu.VMEM((peers, packed, side), F32)),
        flops=flops,
    )
    acts, sums = lax.optimization_barrier((acts, sums))
    sums = exchange(sums, ("xl", "yz"))
    dense = (2, lanes + units, lanes)
    mine, sibling = call(
        grads_kernel,
        (shape(dense, F32), shape(dense, BF16)),
        (acts, all_tokens, all_cotangent),
        flops=flops,
    )
    tile_shape = (slots, side, side)
    own_grad, *far_grads = call(
        pair_kernel,
        (shape(dense[1:], F32),) + (shape(tile_shape, BF16),) * 3,
        (far_index, far_counts, mine, swap(sibling, "core")),
        smem=2,
    )
    far_grads = swap(jnp.concatenate(far_grads), "xl").reshape(3, *tile_shape)
    gate_grad, up_grad, down_grad = call(
        tiles_kernel,
        (shape(tile_shape, F32),) * 3,
        (tile_index, counts, own_grad, *far_grads),
        smem=2,
    )
    output, input_grad = call(finish_kernel, (shape((rows, lanes), BF16),) * 2, (sums,))
    return (output, input_grad, gate_grad, up_grad, down_grad)


def solution(mesh):
    row_size, col_size = mesh.shape["row"], mesh.shape["col"]
    split = Mesh(
        mesh.devices.reshape(row_size // 4, 2, 2, col_size // 2, 2),
        ("xh", "xl", "yl", "yz", "core"),
    )
    row, col = ("xh", "xl", "yl"), ("yz", "core")
    blocks = P(col, row)
    tiles = P(row, col, None)
    small = P(None, row, col)
    return jax.shard_map(
        body,
        mesh=split,
        in_specs=(blocks, blocks, tiles, tiles, tiles, small, small),
        out_specs=(blocks, blocks, tiles, tiles, tiles),
        check_vma=False,
    )
```

```python
import jax
import jax.numpy as jnp
from jax import lax
from jax.experimental import pallas as pl
from jax.experimental.pallas import tpu as pltpu
from jax.sharding import Mesh
from jax.sharding import PartitionSpec as P

LONG = 1 << 36
F32 = jnp.float32
BF16 = jnp.bfloat16
VMEM = pl.BlockSpec(memory_space=pltpu.VMEM)
SMEM = pl.BlockSpec(memory_space=pltpu.SMEM)
NT = (((1,), (1,)), ((), ()))
TN = (((0,), (0,)), ((), ()))


def dot(left, right, dims=None):
    if dims is None:
        return jnp.dot(left, right, preferred_element_type=F32)
    return lax.dot_general(left, right, dims, preferred_element_type=F32)


def place_tiles(dense, tiles, index, counts, which, row_offset, col_offset):
    side = tiles.shape[-1]
    for slot in range(tiles.shape[0]):

        @pl.when(slot < counts[which])
        def _():
            row = pl.multiple_of(index[which, 0, slot] * side + row_offset, side)
            col = pl.multiple_of(index[which, 1, slot] * side + col_offset, side)
            dense[pl.ds(row, side), pl.ds(col, side)] = tiles[slot]


def weights_kernel(index, counts, gate, up, down, dense):
    lanes = dense.shape[1]
    dense[...] = jnp.zeros_like(dense)
    place_tiles(dense, gate, index, counts, 0, 0, 0)
    place_tiles(dense, up, index, counts, 1, 0, lanes // 2)
    place_tiles(dense, down, index, counts, 2, lanes, 0)


def take_tiles(outs, index, counts, read):
    for which, out in enumerate(outs):
        slots, side, _ = out.shape
        for slot in range(slots):
            live = slot < counts[which]

            @pl.when(live)
            def _():
                row = pl.multiple_of(index[which, 0, slot] * side, side)
                col = pl.multiple_of(index[which, 1, slot] * side, side)
                out[slot] = read(which, slot, row, col)

            @pl.when(jnp.logical_not(live))
            def _():
                out[slot] = jnp.zeros(out.shape[1:], out.dtype)


def place(which, row, col, lanes, side):
    row = pl.multiple_of(row + (lanes if which == 2 else 0), side)
    col = pl.multiple_of(col + (lanes // 2 if which == 1 else 0), side)
    return pl.ds(row, side), pl.ds(col, side)


def pair_kernel(far_index, far_counts, mine, received, gate_out, up_out, down_out):
    lanes = mine.shape[1]

    def read(which, slot, row, col):
        at = place(which, row, col, lanes, gate_out.shape[-1])
        return (mine[at] + received[at].astype(F32)).astype(gate_out.dtype)

    take_tiles((gate_out, up_out, down_out), far_index, far_counts, read)


def tiles_kernel(
    index, counts, mine, received, gate_far, up_far, down_far, gate_out, up_out, down_out
):
    lanes = mine.shape[1]
    far = (gate_far, up_far, down_far)

    def read(which, slot, row, col):
        at = place(which, row, col, lanes, gate_out.shape[-1])
        return mine[at] + received[at].astype(F32) + far[which][slot].astype(F32)

    take_tiles((gate_out, up_out, down_out), index, counts, read)


def spread_kernel(tokens, cotangent, out, stage):
    rows, lanes = tokens.shape
    side = out.shape[-1]
    chunks = lanes // side
    part = rows // 2
    peers = out.shape[0] // 2
    size = 2 * chunks * part
    for start, block in ((0, tokens), (chunks, cotangent)):
        for q in range(chunks):
            piece = block[:, q * side : (q + 1) * side].astype(F32)
            for group in range(2):
                row = group * size + (start + q) * part
                stage[row : row + part, :] = piece[group * part : (group + 1) * part]
    for group in range(2):
        packed = stage[group * size : (group + 1) * size, :].astype(out.dtype)
        for peer in range(peers):
            out[group * peers + peer] = packed


def unpack_kernel(me, blocks, tokens, cotangent, stage):
    _, quarter, lanes = tokens.shape
    side = blocks.shape[-1]
    peers = blocks.shape[0] // 2
    rows = quarter // peers
    chunks = lanes // side
    for group in range(2):
        base = (me[0] if group == 0 else 1 - me[0]) * peers
        for peer in range(peers):
            block = blocks[base + peer].astype(F32)
            for q in range(2 * chunks):
                stage[group, peer * rows : (peer + 1) * rows, q * side : (q + 1) * side] = block[
                    q * rows : (q + 1) * rows
                ]
        tokens[group] = stage[group, :, 0:lanes].astype(tokens.dtype)
        cotangent[group] = stage[group, :, lanes:].astype(cotangent.dtype)


def partial_kernel(tokens, cotangent, own, far, own_core, far_core, out):
    _, quarter, lanes = tokens.shape
    for start, near, other in ((0, own, far), (quarter, own_core, far_core)):
        rows = slice(start, start + quarter)
        out[rows, 0:lanes] = (
            dot(tokens[0], near[0:lanes, :]) + dot(tokens[1], other[0:lanes, :])
        ).astype(out.dtype)
        out[rows, lanes:] = (
            dot(cotangent[0], near[lanes:, :], NT) + dot(cotangent[1], other[lanes:, :], NT)
        ).astype(out.dtype)


def sum_parts(parts, start, stop):
    total = parts[start].astype(F32)
    for peer in range(start + 1, stop):
        total = total + parts[peer].astype(F32)
    return total


def units_kernel(parts, out):
    total = sum_parts(parts, 0, parts.shape[0])
    units = total.shape[1] // 3
    gate_sum = total[:, 0:units]
    up_sum = total[:, units : 2 * units]
    hidden_grad = total[:, 2 * units :]
    sigmoid_gate = jax.nn.sigmoid(gate_sum)
    active = gate_sum * sigmoid_gate
    hidden = (active * up_sum).astype(out.dtype)
    gate_act = (
        hidden_grad * up_sum * sigmoid_gate * (1.0 + gate_sum * (1.0 - sigmoid_gate))
    ).astype(out.dtype)
    up_act = (hidden_grad * active).astype(out.dtype)
    for peer in range(out.shape[0]):
        out[peer, :, 0:units] = hidden
        out[peer, :, units : 2 * units] = gate_act
        out[peer, :, 2 * units :] = up_act


def apply_kernel(me, acts, own, far, own_core, far_core, out, result, stage):
    quarter = result.shape[0]
    lanes = own.shape[1]
    units = own.shape[0] - lanes
    peers = out.shape[0] // 2
    side = out.shape[-1]
    rows = quarter // peers
    near, other = slice(0, quarter), slice(quarter, 2 * quarter)
    for group, first, second in ((0, own, own_core), (1, far, far_core)):
        result[:, 0:lanes] = dot(acts[near, 0:units], first[lanes:, :]) + dot(
            acts[other, 0:units], second[lanes:, :]
        )
        result[:, lanes:] = dot(acts[near, units:], first[0:lanes, :], NT) + dot(
            acts[other, units:], second[0:lanes, :], NT
        )
        base = (me[0] if group == 0 else 1 - me[0]) * peers
        for peer in range(peers):
            for q in range(2 * lanes // side):
                stage[peer, q * rows : (q + 1) * rows, :] = result[
                    peer * rows : (peer + 1) * rows, q * side : (q + 1) * side
                ]
            out[base + peer] = stage[peer].astype(out.dtype)


def grads_kernel(acts, tokens, cotangent, own, far, own_core, far_core):
    _, quarter, lanes = tokens.shape
    units = own.shape[0] - lanes
    for group, start, out in (
        (1, quarter, far_core),
        (1, 0, far),
        (0, quarter, own_core),
        (0, 0, own),
    ):
        rows = slice(start, start + quarter)
        out[0:lanes, :] = dot(tokens[group], acts[rows, units:], TN).astype(out.dtype)
        out[lanes:, :] = dot(acts[rows, 0:units], cotangent[group], TN).astype(out.dtype)


def finish_kernel(parts, output, input_grad):
    rows, lanes = output.shape
    part = rows // 2
    peers = parts.shape[0] // 2
    side = parts.shape[-1]
    chunks = lanes // side
    for group in range(2):
        total = sum_parts(parts, group * peers, (group + 1) * peers)
        for start, out in ((0, output), (chunks, input_grad)):
            for q in range(chunks):
                piece = total[(start + q) * part : (start + q + 1) * part]
                out[group * part : (group + 1) * part, q * side : (q + 1) * side] = piece.astype(
                    out.dtype
                )


def call(kernel, outs, args, smem=0, scratch=(), flops=0, limit=20 << 20):
    moved = sum(a.size * a.dtype.itemsize for a in args) + sum(
        o.size * jnp.dtype(o.dtype).itemsize for o in outs
    )
    single = len(outs) == 1
    return pl.pallas_call(
        kernel,
        out_shape=outs[0] if single else outs,
        in_specs=(SMEM,) * smem + (VMEM,) * (len(args) - smem),
        out_specs=VMEM if single else (VMEM,) * len(outs),
        scratch_shapes=scratch,
        compiler_params=pltpu.CompilerParams(vmem_limit_bytes=limit),
        cost_estimate=pl.CostEstimate(flops=flops, bytes_accessed=moved, transcendentals=0),
    )(*args)


def exchange(blocks, axis):
    return lax.all_to_all(blocks, axis, split_axis=0, concat_axis=0, tiled=True)


def swap(block, axis):
    return lax.ppermute(block, axis, [(0, 1), (1, 0)])


def body(tokens, cotangent, gate_tiles, up_tiles, down_tiles, tile_index, tile_counts):
    rows, lanes = tokens.shape
    slots, side, _ = gate_tiles.shape
    row_peers = lax.axis_size("xh") * lax.axis_size("yl")
    peers = lax.axis_size("yz")
    units = 2 * side
    quarter = peers * rows // 2
    share = 2 * quarter // row_peers
    packed = lanes // side * rows
    flops = 24 * quarter * lanes * units
    counts = tile_counts.reshape(3)
    index = tile_index.transpose(0, 2, 1)
    me = lax.axis_index("xl").astype(jnp.int32).reshape(1)
    shape = jax.ShapeDtypeStruct

    spread = call(
        spread_kernel,
        (shape((2 * peers, packed, side), BF16),),
        (tokens, cotangent),
        scratch=(pltpu.VMEM((2 * packed, side), F32),),
        limit=None,
    )
    spread, gate_tiles, up_tiles, down_tiles = lax.optimization_barrier(
        (spread, gate_tiles, up_tiles, down_tiles)
    )
    blocks = exchange(spread, ("xl", "yz"))
    own = call(
        weights_kernel,
        (shape((lanes + units, lanes), BF16),),
        (index, counts, gate_tiles, up_tiles, down_tiles),
        smem=2,
        limit=None,
    )
    far = swap(own, "xl")
    own_core = swap(own, "core")
    far_core = swap(far, "core")
    listing = jnp.concatenate([index.reshape(3, 2 * slots), counts[:, None]], axis=1)
    listing = swap(listing, "xl")
    far_core, listing = lax.optimization_barrier((far_core, listing))
    far_index = listing[:, 0 : 2 * slots].reshape(3, 2, slots)
    far_counts = listing[:, 2 * slots]
    weights = (own, far, own_core, far_core)
    all_tokens, all_cotangent = call(
        unpack_kernel,
        (shape((2, quarter, lanes), BF16),) * 2,
        (me, blocks),
        smem=1,
        scratch=(pltpu.VMEM((2, quarter, 2 * lanes), F32),),
        flops=LONG,
    )
    parts = call(
        partial_kernel,
        (shape((2 * quarter, 3 * units), BF16),),
        (all_tokens, all_cotangent, *weights),
        flops=flops,
    )
    parts = exchange(parts.reshape(row_peers, share, 3 * units), ("xh", "yl"))
    acts = call(units_kernel, (shape(parts.shape, BF16),), (parts,))
    acts = exchange(acts, ("xh", "yl")).reshape(2 * quarter, 3 * units)
    sums = call(
        apply_kernel,
        (shape((2 * peers, packed, side), BF16),),
        (me, acts, *weights),
        smem=1,
        scratch=(pltpu.VMEM((quarter, 2 * lanes), F32), pltpu.VMEM((peers, packed, side), F32)),
        flops=flops,
    )
    acts, sums = lax.optimization_barrier((acts, sums))
    sums = exchange(sums, ("xl", "yz"))
    dense = (lanes + units, lanes)
    own_grad, far_grad, own_core, far_core = call(
        grads_kernel,
        (shape(dense, F32),) * 2 + (shape(dense, BF16),) * 2,
        (acts, all_tokens, all_cotangent),
        flops=flops,
    )
    tile_shape = (slots, side, side)
    far_grads = call(
        pair_kernel,
        (shape(tile_shape, BF16),) * 3,
        (far_index, far_counts, far_grad, swap(far_core, "core")),
        smem=2,
    )
    far_grads = swap(jnp.concatenate(far_grads), "xl").reshape(3, *tile_shape)
    gate_grad, up_grad, down_grad = call(
        tiles_kernel,
        (shape(tile_shape, F32),) * 3,
        (index, counts, own_grad, swap(own_core, "core"), *far_grads),
        smem=2,
    )
    output, input_grad = call(finish_kernel, (shape((rows, lanes), BF16),) * 2, (sums,), flops=LONG)
    return (output, input_grad, gate_grad, up_grad, down_grad)


def solution(mesh):
    row_size, col_size = mesh.shape["row"], mesh.shape["col"]
    split = Mesh(
        mesh.devices.reshape(row_size // 4, 2, 2, col_size // 2, 2),
        ("xh", "xl", "yl", "yz", "core"),
    )
    row, col = ("xh", "xl", "yl"), ("yz", "core")
    blocks = P(col, row)
    tiles = P(row, col, None)
    small = P(None, row, col)
    return jax.shard_map(
        body,
        mesh=split,
        in_specs=(blocks, blocks, tiles, tiles, tiles, small, small),
        out_specs=(blocks, blocks, tiles, tiles, tiles),
        check_vma=False,
    )
```

```python
import jax
import jax.numpy as jnp
from jax import lax
from jax.experimental import pallas as pl
from jax.experimental.pallas import tpu as pltpu
from jax.sharding import Mesh
from jax.sharding import PartitionSpec as P

LONG = 1 << 36
UNPACK = 0
F32 = jnp.float32
BF16 = jnp.bfloat16
VMEM = pl.BlockSpec(memory_space=pltpu.VMEM)
SMEM = pl.BlockSpec(memory_space=pltpu.SMEM)
NT = (((1,), (1,)), ((), ()))
TN = (((0,), (0,)), ((), ()))


def dot(left, right, dims=None):
    if dims is None:
        return jnp.dot(left, right, preferred_element_type=F32)
    return lax.dot_general(left, right, dims, preferred_element_type=F32)


def place_tiles(dense, tiles, index, counts, which, row_offset, col_offset):
    side = tiles.shape[-1]
    for slot in range(tiles.shape[0]):

        @pl.when(slot < counts[which])
        def _():
            row = pl.multiple_of(index[which, 0, slot] * side + row_offset, side)
            col = pl.multiple_of(index[which, 1, slot] * side + col_offset, side)
            dense[pl.ds(row, side), pl.ds(col, side)] = tiles[slot]


def weights_kernel(index, counts, gate, up, down, dense):
    lanes = dense.shape[1]
    dense[...] = jnp.zeros_like(dense)
    place_tiles(dense, gate, index, counts, 0, 0, 0)
    place_tiles(dense, up, index, counts, 1, 0, lanes // 2)
    place_tiles(dense, down, index, counts, 2, lanes, 0)


def take_tiles(outs, index, counts, read):
    for which, out in enumerate(outs):
        slots, side, _ = out.shape
        for slot in range(slots):
            live = slot < counts[which]

            @pl.when(live)
            def _():
                row = pl.multiple_of(index[which, 0, slot] * side, side)
                col = pl.multiple_of(index[which, 1, slot] * side, side)
                out[slot] = read(which, slot, row, col)

            @pl.when(jnp.logical_not(live))
            def _():
                out[slot] = jnp.zeros(out.shape[1:], out.dtype)


def place(which, row, col, lanes, side):
    row = pl.multiple_of(row + (lanes if which == 2 else 0), side)
    col = pl.multiple_of(col + (lanes // 2 if which == 1 else 0), side)
    return pl.ds(row, side), pl.ds(col, side)


def tiles_kernel(index, counts, own, received, gate_out, up_out, down_out):
    lanes = own.shape[1]

    def read(which, slot, row, col):
        at = place(which, row, col, lanes, gate_out.shape[-1])
        return own[at] + received[at].astype(F32)

    take_tiles((gate_out, up_out, down_out), index, counts, read)


def spread_kernel(tokens, cotangent, out, stage):
    rows, lanes = tokens.shape
    side = out.shape[-1]
    chunks = lanes // side
    part = rows // 2
    peers = out.shape[0] // 2
    size = 2 * chunks * part
    for start, block in ((0, tokens), (chunks, cotangent)):
        for q in range(chunks):
            piece = block[:, q * side : (q + 1) * side].astype(F32)
            for group in range(2):
                row = group * size + (start + q) * part
                stage[row : row + part, :] = piece[group * part : (group + 1) * part]
    for group in range(2):
        packed = stage[group * size : (group + 1) * size, :].astype(out.dtype)
        for peer in range(peers):
            out[group * peers + peer] = packed


def unpack_kernel(me, blocks, own, far, stage):
    _, quarter, lanes = own.shape
    side = blocks.shape[-1]
    peers = blocks.shape[0] // 2
    rows = quarter // peers
    chunks = lanes // side
    for group, out in ((0, own), (1, far)):
        base = (me[0] if group == 0 else 1 - me[0]) * peers
        for peer in range(peers):
            block = blocks[base + peer].astype(F32)
            for q in range(2 * chunks):
                stage[group, peer * rows : (peer + 1) * rows, q * side : (q + 1) * side] = block[
                    q * rows : (q + 1) * rows
                ]
        out[0] = stage[group, :, 0:lanes].astype(out.dtype)
        out[1] = stage[group, :, lanes:].astype(out.dtype)


def partial_kernel(own_rows, far_rows, own, far, own_core, far_core, out):
    _, quarter, lanes = own_rows.shape
    for start, near, other in ((0, own, far), (quarter, own_core, far_core)):
        rows = slice(start, start + quarter)
        out[rows, 0:lanes] = (
            dot(own_rows[0], near[0:lanes, :]) + dot(far_rows[0], other[0:lanes, :])
        ).astype(out.dtype)
        out[rows, lanes:] = (
            dot(own_rows[1], near[lanes:, :], NT) + dot(far_rows[1], other[lanes:, :], NT)
        ).astype(out.dtype)


def sum_parts(parts, start, stop):
    total = parts[start].astype(F32)
    for peer in range(start + 1, stop):
        total = total + parts[peer].astype(F32)
    return total


def units_kernel(parts, out):
    total = sum_parts(parts, 0, parts.shape[0])
    units = total.shape[1] // 3
    gate_sum = total[:, 0:units]
    up_sum = total[:, units : 2 * units]
    hidden_grad = total[:, 2 * units :]
    sigmoid_gate = jax.nn.sigmoid(gate_sum)
    active = gate_sum * sigmoid_gate
    hidden = (active * up_sum).astype(out.dtype)
    gate_act = (
        hidden_grad * up_sum * sigmoid_gate * (1.0 + gate_sum * (1.0 - sigmoid_gate))
    ).astype(out.dtype)
    up_act = (hidden_grad * active).astype(out.dtype)
    for peer in range(out.shape[0]):
        out[peer, :, 0:units] = hidden
        out[peer, :, units : 2 * units] = gate_act
        out[peer, :, 2 * units :] = up_act


def apply_kernel(me, acts, own, far, own_core, far_core, out, result, stage):
    quarter = result.shape[0]
    lanes = own.shape[1]
    units = own.shape[0] - lanes
    peers = out.shape[0] // 2
    side = out.shape[-1]
    rows = quarter // peers
    near, other = slice(0, quarter), slice(quarter, 2 * quarter)
    for group, first, second in ((0, own, own_core), (1, far, far_core)):
        result[:, 0:lanes] = dot(acts[near, 0:units], first[lanes:, :]) + dot(
            acts[other, 0:units], second[lanes:, :]
        )
        result[:, lanes:] = dot(acts[near, units:], first[0:lanes, :], NT) + dot(
            acts[other, units:], second[0:lanes, :], NT
        )
        base = (me[0] if group == 0 else 1 - me[0]) * peers
        for peer in range(peers):
            for q in range(2 * lanes // side):
                stage[peer, q * rows : (q + 1) * rows, :] = result[
                    peer * rows : (peer + 1) * rows, q * side : (q + 1) * side
                ]
            out[base + peer] = stage[peer].astype(out.dtype)


def grads_kernel(acts, far_acts, own_rows, far_rows, own, sibling):
    _, quarter, lanes = own_rows.shape
    units = own.shape[0] - lanes
    for start, out in ((quarter, sibling), (0, own)):
        rows = slice(start, start + quarter)
        out[0:lanes, :] = (
            dot(own_rows[0], acts[rows, units:], TN) + dot(far_rows[0], far_acts[rows, units:], TN)
        ).astype(out.dtype)
        out[lanes:, :] = (
            dot(acts[rows, 0:units], own_rows[1], TN)
            + dot(far_acts[rows, 0:units], far_rows[1], TN)
        ).astype(out.dtype)


def finish_kernel(parts, output, input_grad):
    rows, lanes = output.shape
    part = rows // 2
    peers = parts.shape[0] // 2
    side = parts.shape[-1]
    chunks = lanes // side
    for group in range(2):
        total = sum_parts(parts, group * peers, (group + 1) * peers)
        for start, out in ((0, output), (chunks, input_grad)):
            for q in range(chunks):
                piece = total[(start + q) * part : (start + q + 1) * part]
                out[group * part : (group + 1) * part, q * side : (q + 1) * side] = piece.astype(
                    out.dtype
                )


def call(kernel, outs, args, smem=0, scratch=(), flops=0, limit=12 << 20):
    moved = sum(a.size * a.dtype.itemsize for a in args) + sum(
        o.size * jnp.dtype(o.dtype).itemsize for o in outs
    )
    single = len(outs) == 1
    return pl.pallas_call(
        kernel,
        out_shape=outs[0] if single else outs,
        in_specs=(SMEM,) * smem + (VMEM,) * (len(args) - smem),
        out_specs=VMEM if single else (VMEM,) * len(outs),
        scratch_shapes=scratch,
        compiler_params=pltpu.CompilerParams(vmem_limit_bytes=limit),
        cost_estimate=pl.CostEstimate(flops=flops, bytes_accessed=moved, transcendentals=0),
    )(*args)


def exchange(blocks, axis):
    return lax.all_to_all(blocks, axis, split_axis=0, concat_axis=0, tiled=True)


def swap(block, axis):
    return lax.ppermute(block, axis, [(0, 1), (1, 0)])


def body(tokens, cotangent, gate_tiles, up_tiles, down_tiles, tile_index, tile_counts):
    rows, lanes = tokens.shape
    slots, side, _ = gate_tiles.shape
    row_peers = lax.axis_size("xh") * lax.axis_size("yl")
    peers = lax.axis_size("yz")
    units = 2 * side
    quarter = peers * rows // 2
    share = 2 * quarter // row_peers
    packed = lanes // side * rows
    flops = 24 * quarter * lanes * units
    counts = tile_counts.reshape(3)
    index = tile_index.transpose(0, 2, 1)
    me = lax.axis_index("xl").astype(jnp.int32).reshape(1)
    shape = jax.ShapeDtypeStruct

    spread = call(
        spread_kernel,
        (shape((2 * peers, packed, side), BF16),),
        (tokens, cotangent),
        scratch=(pltpu.VMEM((2 * packed, side), F32),),
        limit=None,
    )
    spread, gate_tiles, up_tiles, down_tiles = lax.optimization_barrier(
        (spread, gate_tiles, up_tiles, down_tiles)
    )
    blocks = exchange(spread, ("xl", "yz"))
    own = call(
        weights_kernel,
        (shape((lanes + units, lanes), BF16),),
        (index, counts, gate_tiles, up_tiles, down_tiles),
        smem=2,
        limit=None,
    )
    far = swap(own, "xl")
    own_core = swap(own, "core")
    far_core = swap(far, "core")
    weights = (own, far, own_core, far_core)
    own_rows, far_rows = call(
        unpack_kernel,
        (shape((2, quarter, lanes), BF16),) * 2,
        (me, blocks),
        smem=1,
        scratch=(pltpu.VMEM((2, quarter, 2 * lanes), F32),),
        flops=UNPACK,
    )
    parts = call(
        partial_kernel,
        (shape((2 * quarter, 3 * units), BF16),),
        (own_rows, far_rows, *weights),
        flops=flops,
    )
    parts = exchange(parts.reshape(row_peers, share, 3 * units), ("xh", "yl"))
    acts = call(units_kernel, (shape(parts.shape, BF16),), (parts,))
    acts = exchange(acts, ("xh", "yl")).reshape(2 * quarter, 3 * units)
    sums = call(
        apply_kernel,
        (shape((2 * peers, packed, side), BF16),),
        (me, acts, *weights),
        smem=1,
        scratch=(pltpu.VMEM((quarter, 2 * lanes), F32), pltpu.VMEM((peers, packed, side), F32)),
        flops=flops,
    )
    sums = exchange(sums, ("xl", "yz"))
    far_acts, far_rows = swap(acts, "xl"), swap(far_rows, "xl")
    dense = (lanes + units, lanes)
    own_grad, sibling_grad = call(
        grads_kernel,
        (shape(dense, F32), shape(dense, BF16)),
        (acts, far_acts, own_rows, far_rows),
        flops=flops,
    )
    gate_grad, up_grad, down_grad = call(
        tiles_kernel,
        (shape((slots, side, side), F32),) * 3,
        (index, counts, own_grad, swap(sibling_grad, "core")),
        smem=2,
    )
    output, input_grad = call(finish_kernel, (shape((rows, lanes), BF16),) * 2, (sums,), flops=LONG)
    return (output, input_grad, gate_grad, up_grad, down_grad)


def solution(mesh):
    row_size, col_size = mesh.shape["row"], mesh.shape["col"]
    split = Mesh(
        mesh.devices.reshape(row_size // 4, 2, 2, col_size // 2, 2),
        ("xh", "xl", "yl", "yz", "core"),
    )
    row, col = ("xh", "xl", "yl"), ("yz", "core")
    blocks = P(col, row)
    tiles = P(row, col, None)
    small = P(None, row, col)
    return jax.shard_map(
        body,
        mesh=split,
        in_specs=(blocks, blocks, tiles, tiles, tiles, small, small),
        out_specs=(blocks, blocks, tiles, tiles, tiles),
        check_vma=False,
    )
```

```python
import functools

import jax
import jax.numpy as jnp
from jax import lax
from jax.experimental import pallas as pl
from jax.experimental.pallas import tpu as pltpu
from jax.sharding import Mesh
from jax.sharding import PartitionSpec as P

LONG = 1 << 36
UNPACK = 0
ADD = 0
YH = 4
F32 = jnp.float32
BF16 = jnp.bfloat16
VMEM = pl.BlockSpec(memory_space=pltpu.VMEM)
SMEM = pl.BlockSpec(memory_space=pltpu.SMEM)
NT = (((1,), (1,)), ((), ()))
TN = (((0,), (0,)), ((), ()))


def dot(left, right, dims=None):
    if dims is None:
        return jnp.dot(left, right, preferred_element_type=F32)
    return lax.dot_general(left, right, dims, preferred_element_type=F32)


def place_tiles(dense, tiles, index, counts, which, row_offset, col_offset):
    side = tiles.shape[-1]
    for slot in range(tiles.shape[0]):

        @pl.when(slot < counts[which])
        def _():
            row = pl.multiple_of(index[which, 0, slot] * side + row_offset, side)
            col = pl.multiple_of(index[which, 1, slot] * side + col_offset, side)
            dense[pl.ds(row, side), pl.ds(col, side)] = tiles[slot]


def take_tiles(outs, index, counts, read):
    for which, out in enumerate(outs):
        slots, side, _ = out.shape
        for slot in range(slots):
            live = slot < counts[which]

            @pl.when(live)
            def _():
                row = pl.multiple_of(index[which, 0, slot] * side, side)
                col = pl.multiple_of(index[which, 1, slot] * side, side)
                out[slot] = read(which, slot, row, col)

            @pl.when(jnp.logical_not(live))
            def _():
                out[slot] = jnp.zeros(out.shape[1:], out.dtype)


def place(which, row, col, lanes, side):
    row = pl.multiple_of(row + (lanes if which == 2 else 0), side)
    col = pl.multiple_of(col + (lanes // 2 if which == 1 else 0), side)
    return pl.ds(row, side), pl.ds(col, side)


def tiles_kernel(index, counts, own, received, gate_out, up_out, down_out):
    lanes = own.shape[1]

    def read(which, slot, row, col):
        at = place(which, row, col, lanes, gate_out.shape[-1])
        return own[at] + received[at].astype(F32)

    take_tiles((gate_out, up_out, down_out), index, counts, read)


def start_kernel(index, counts, tokens, cotangent, gate, up, down, out, dense, stage):
    rows, lanes = tokens.shape
    side = out.shape[-1]
    chunks = lanes // side
    part = rows // 2
    peers = out.shape[0] // 2
    size = 2 * chunks * part
    dense[...] = jnp.zeros_like(dense)
    place_tiles(dense, gate, index, counts, 0, 0, 0)
    place_tiles(dense, up, index, counts, 1, 0, lanes // 2)
    place_tiles(dense, down, index, counts, 2, lanes, 0)
    for start, block in ((0, tokens), (chunks, cotangent)):
        for q in range(chunks):
            piece = block[:, q * side : (q + 1) * side].astype(F32)
            for group in range(2):
                row = group * size + (start + q) * part
                stage[row : row + part, :] = piece[group * part : (group + 1) * part]
    for group in range(2):
        packed = stage[group * size : (group + 1) * size, :].astype(out.dtype)
        for peer in range(peers):
            out[group * peers + peer] = packed


def copies_kernel(block, out):
    for peer in range(out.shape[0]):
        out[peer] = block[...]


def block_at(group, peer, step):
    return (peer // step) * 2 * step + group * step + peer % step


def unpack_kernel(step, me, blocks, own, far, stage):
    _, quarter, lanes = own.shape
    side = blocks.shape[-1]
    peers = blocks.shape[0] // 2
    rows = quarter // peers
    chunks = lanes // side
    for group, out in ((0, own), (1, far)):
        side_of = me[0] if group == 0 else 1 - me[0]
        for peer in range(peers):
            block = blocks[block_at(side_of, peer, step)].astype(F32)
            for q in range(2 * chunks):
                stage[group, peer * rows : (peer + 1) * rows, q * side : (q + 1) * side] = block[
                    q * rows : (q + 1) * rows
                ]
        out[0] = stage[group, :, 0:lanes].astype(out.dtype)
        out[1] = stage[group, :, lanes:].astype(out.dtype)


def partial_kernel(own_rows, far_rows, own, far, own_core, far_core, out):
    _, quarter, lanes = own_rows.shape
    for start, near, other in ((0, own, far), (quarter, own_core, far_core)):
        rows = slice(start, start + quarter)
        out[rows, 0:lanes] = (
            dot(own_rows[0], near[0:lanes, :]) + dot(far_rows[0], other[0:lanes, :])
        ).astype(out.dtype)
        out[rows, lanes:] = (
            dot(own_rows[1], near[lanes:, :], NT) + dot(far_rows[1], other[lanes:, :], NT)
        ).astype(out.dtype)


def sum_parts(parts, start, stop):
    total = parts[start].astype(F32)
    for peer in range(start + 1, stop):
        total = total + parts[peer].astype(F32)
    return total


def units_kernel(parts, out):
    total = sum_parts(parts, 0, parts.shape[0])
    units = total.shape[1] // 3
    gate_sum = total[:, 0:units]
    up_sum = total[:, units : 2 * units]
    hidden_grad = total[:, 2 * units :]
    sigmoid_gate = jax.nn.sigmoid(gate_sum)
    active = gate_sum * sigmoid_gate
    hidden = (active * up_sum).astype(out.dtype)
    gate_act = (
        hidden_grad * up_sum * sigmoid_gate * (1.0 + gate_sum * (1.0 - sigmoid_gate))
    ).astype(out.dtype)
    up_act = (hidden_grad * active).astype(out.dtype)
    for peer in range(out.shape[0]):
        out[peer, :, 0:units] = hidden
        out[peer, :, units : 2 * units] = gate_act
        out[peer, :, 2 * units :] = up_act


def apply_kernel(step, me, acts, own, far, own_core, far_core, out, result, stage):
    quarter = result.shape[0]
    lanes = own.shape[1]
    units = own.shape[0] - lanes
    peers = out.shape[0] // 2
    side = out.shape[-1]
    rows = quarter // peers
    near, other = slice(0, quarter), slice(quarter, 2 * quarter)
    for group, first, second in ((0, own, own_core), (1, far, far_core)):
        result[:, 0:lanes] = dot(acts[near, 0:units], first[lanes:, :]) + dot(
            acts[other, 0:units], second[lanes:, :]
        )
        result[:, lanes:] = dot(acts[near, units:], first[0:lanes, :], NT) + dot(
            acts[other, units:], second[0:lanes, :], NT
        )
        side_of = me[0] if group == 0 else 1 - me[0]
        for peer in range(peers):
            for q in range(2 * lanes // side):
                stage[peer, q * rows : (q + 1) * rows, :] = result[
                    peer * rows : (peer + 1) * rows, q * side : (q + 1) * side
                ]
            out[block_at(side_of, peer, step)] = stage[peer].astype(out.dtype)


def add_kernel(parts, out):
    out[...] = sum_parts(parts, 0, parts.shape[0])


def grads_kernel(acts, far_acts, own_rows, far_rows, own, sibling):
    _, quarter, lanes = own_rows.shape
    units = own.shape[0] - lanes
    for start, out in ((quarter, sibling), (0, own)):
        rows = slice(start, start + quarter)
        out[0:lanes, :] = (
            dot(own_rows[0], acts[rows, units:], TN) + dot(far_rows[0], far_acts[rows, units:], TN)
        ).astype(out.dtype)
        out[lanes:, :] = (
            dot(acts[rows, 0:units], own_rows[1], TN)
            + dot(far_acts[rows, 0:units], far_rows[1], TN)
        ).astype(out.dtype)


def finish_kernel(parts, output, input_grad):
    rows, lanes = output.shape
    part = rows // 2
    peers = parts.shape[0] // 2
    side = parts.shape[-1]
    chunks = lanes // side
    for group in range(2):
        total = sum_parts(parts, group * peers, (group + 1) * peers)
        for start, out in ((0, output), (chunks, input_grad)):
            for q in range(chunks):
                piece = total[(start + q) * part : (start + q + 1) * part]
                out[group * part : (group + 1) * part, q * side : (q + 1) * side] = piece.astype(
                    out.dtype
                )


def call(kernel, outs, args, smem=0, scratch=(), flops=0, limit=12 << 20):
    moved = sum(a.size * a.dtype.itemsize for a in args) + sum(
        o.size * jnp.dtype(o.dtype).itemsize for o in outs
    )
    single = len(outs) == 1
    return pl.pallas_call(
        kernel,
        out_shape=outs[0] if single else outs,
        in_specs=(SMEM,) * smem + (VMEM,) * (len(args) - smem),
        out_specs=VMEM if single else (VMEM,) * len(outs),
        scratch_shapes=scratch,
        compiler_params=pltpu.CompilerParams(vmem_limit_bytes=limit),
        cost_estimate=pl.CostEstimate(flops=flops, bytes_accessed=moved, transcendentals=0),
    )(*args)


def exchange(blocks, axis):
    return lax.all_to_all(blocks, axis, split_axis=0, concat_axis=0, tiled=True)


def swap(block, axis):
    return lax.ppermute(block, axis, [(0, 1), (1, 0)])


def body(tokens, cotangent, gate_tiles, up_tiles, down_tiles, tile_index, tile_counts):
    rows, lanes = tokens.shape
    slots, side, _ = gate_tiles.shape
    row_peers = lax.axis_size("xh") * lax.axis_size("yl")
    step, depth = lax.axis_size("yh"), lax.axis_size("z")
    peers = step * depth
    units = 2 * side
    quarter = peers * rows // 2
    share = 2 * quarter // row_peers
    packed = lanes // side * rows
    flops = 24 * quarter * lanes * units
    counts = tile_counts.reshape(3)
    index = tile_index.transpose(0, 2, 1)
    me = lax.axis_index("xl").astype(jnp.int32).reshape(1)
    shape = jax.ShapeDtypeStruct

    dense = (lanes + units, lanes)
    spread, own = call(
        start_kernel,
        (shape((2 * step, packed, side), BF16), shape(dense, BF16)),
        (index, counts, tokens, cotangent, gate_tiles, up_tiles, down_tiles),
        smem=2,
        scratch=(pltpu.VMEM((2 * packed, side), F32),),
        limit=None,
    )
    blocks = exchange(spread, ("xl", "yh")).reshape(2 * step * packed, side)
    blocks = call(copies_kernel, (shape((depth, *blocks.shape), BF16),), (blocks,))
    blocks = exchange(blocks, "z").reshape(2 * peers, packed, side)
    far = swap(own, "xl")
    own_core = swap(own, "core")
    far_core = swap(far, "core")
    weights = (own, far, own_core, far_core)
    own_rows, far_rows = call(
        functools.partial(unpack_kernel, step),
        (shape((2, quarter, lanes), BF16),) * 2,
        (me, blocks),
        smem=1,
        scratch=(pltpu.VMEM((2, quarter, 2 * lanes), F32),),
        flops=UNPACK,
    )
    parts = call(
        partial_kernel,
        (shape((2 * quarter, 3 * units), BF16),),
        (own_rows, far_rows, *weights),
        flops=flops,
    )
    parts = exchange(parts.reshape(row_peers, share, 3 * units), ("xh", "yl"))
    acts = call(units_kernel, (shape(parts.shape, BF16),), (parts,))
    acts = exchange(acts, ("xh", "yl")).reshape(2 * quarter, 3 * units)
    sums = call(
        functools.partial(apply_kernel, step),
        (shape((2 * peers, packed, side), BF16),),
        (me, acts, *weights),
        smem=1,
        scratch=(pltpu.VMEM((quarter, 2 * lanes), F32), pltpu.VMEM((peers, packed, side), F32)),
        flops=flops,
    )
    sums = exchange(sums.reshape(depth, 2 * step * packed, side), "z")
    sums = call(add_kernel, (shape(sums.shape[1:], F32),), (sums,), flops=ADD)
    sums = exchange(sums.reshape(2 * step, packed, side), ("xl", "yh"))
    far_acts, far_rows = swap(acts, "xl"), swap(far_rows, "xl")
    own_grad, sibling_grad = call(
        grads_kernel,
        (shape(dense, F32), shape(dense, BF16)),
        (acts, far_acts, own_rows, far_rows),
        flops=flops,
    )
    output, input_grad = call(finish_kernel, (shape((rows, lanes), BF16),) * 2, (sums,), flops=LONG)
    index, output, input_grad = lax.optimization_barrier((index, output, input_grad))
    gate_grad, up_grad, down_grad = call(
        tiles_kernel,
        (shape((slots, side, side), F32),) * 3,
        (index, counts, own_grad, swap(sibling_grad, "core")),
        smem=2,
    )
    return (output, input_grad, gate_grad, up_grad, down_grad)


def solution(mesh):
    row_size, col_size = mesh.shape["row"], mesh.shape["col"]
    split = Mesh(
        mesh.devices.reshape(row_size // 4, 2, 2, YH, col_size // (2 * YH), 2),
        ("xh", "xl", "yl", "yh", "z", "core"),
    )
    row, col = ("xh", "xl", "yl"), ("yh", "z", "core")
    blocks = P(col, row)
    tiles = P(row, col, None)
    small = P(None, row, col)
    return jax.shard_map(
        body,
        mesh=split,
        in_specs=(blocks, blocks, tiles, tiles, tiles, small, small),
        out_specs=(blocks, blocks, tiles, tiles, tiles),
        check_vma=False,
    )
```

```python
import jax
import jax.numpy as jnp
from jax import lax
from jax.experimental import pallas as pl
from jax.experimental.pallas import tpu as pltpu
from jax.sharding import Mesh
from jax.sharding import PartitionSpec as P

LONG = 1 << 36
UNPACK = 0
F32 = jnp.float32
BF16 = jnp.bfloat16
VMEM = pl.BlockSpec(memory_space=pltpu.VMEM)
SMEM = pl.BlockSpec(memory_space=pltpu.SMEM)
NT = (((1,), (1,)), ((), ()))
TN = (((0,), (0,)), ((), ()))


def dot(left, right, dims=None):
    if dims is None:
        return jnp.dot(left, right, preferred_element_type=F32)
    return lax.dot_general(left, right, dims, preferred_element_type=F32)


def place_tiles(dense, tiles, index, counts, which, row_offset, col_offset):
    side = tiles.shape[-1]
    for slot in range(tiles.shape[0]):

        @pl.when(slot < counts[which])
        def _():
            row = pl.multiple_of(index[which, 0, slot] * side + row_offset, side)
            col = pl.multiple_of(index[which, 1, slot] * side + col_offset, side)
            dense[pl.ds(row, side), pl.ds(col, side)] = tiles[slot]


def take_tiles(outs, index, counts, read):
    for which, out in enumerate(outs):
        slots, side, _ = out.shape
        for slot in range(slots):
            live = slot < counts[which]

            @pl.when(live)
            def _():
                row = pl.multiple_of(index[which, 0, slot] * side, side)
                col = pl.multiple_of(index[which, 1, slot] * side, side)
                out[slot] = read(which, slot, row, col)

            @pl.when(jnp.logical_not(live))
            def _():
                out[slot] = jnp.zeros(out.shape[1:], out.dtype)


def place(which, row, col, lanes, side):
    row = pl.multiple_of(row + (lanes if which == 2 else 0), side)
    col = pl.multiple_of(col + (lanes // 2 if which == 1 else 0), side)
    return pl.ds(row, side), pl.ds(col, side)


def tiles_kernel(index, counts, own, received, gate_out, up_out, down_out):
    lanes = own.shape[1]

    def read(which, slot, row, col):
        at = place(which, row, col, lanes, gate_out.shape[-1])
        return own[at] + received[at].astype(F32)

    take_tiles((gate_out, up_out, down_out), index, counts, read)


def start_kernel(index, counts, tokens, cotangent, gate, up, down, out, dense, stage):
    rows, lanes = tokens.shape
    side = out.shape[-1]
    chunks = lanes // side
    part = rows // 2
    peers = out.shape[0] // 2
    size = 2 * chunks * part
    dense[...] = jnp.zeros_like(dense)
    place_tiles(dense, gate, index, counts, 0, 0, 0)
    place_tiles(dense, up, index, counts, 1, 0, lanes // 2)
    place_tiles(dense, down, index, counts, 2, lanes, 0)
    for start, block in ((0, tokens), (chunks, cotangent)):
        for q in range(chunks):
            piece = block[:, q * side : (q + 1) * side].astype(F32)
            for group in range(2):
                row = group * size + (start + q) * part
                stage[row : row + part, :] = piece[group * part : (group + 1) * part]
    for group in range(2):
        packed = stage[group * size : (group + 1) * size, :].astype(out.dtype)
        for peer in range(peers):
            out[group * peers + peer] = packed


def unpack_kernel(me, blocks, own, far, stage):
    _, quarter, lanes = own.shape
    side = blocks.shape[-1]
    peers = blocks.shape[0] // 2
    rows = quarter // peers
    chunks = lanes // side
    for group, out in ((0, own), (1, far)):
        base = (me[0] if group == 0 else 1 - me[0]) * peers
        for peer in range(peers):
            block = blocks[base + peer].astype(F32)
            for q in range(2 * chunks):
                stage[group, peer * rows : (peer + 1) * rows, q * side : (q + 1) * side] = block[
                    q * rows : (q + 1) * rows
                ]
        out[0] = stage[group, :, 0:lanes].astype(out.dtype)
        out[1] = stage[group, :, lanes:].astype(out.dtype)


def partial_kernel(own_rows, far_rows, own, far, own_core, far_core, out):
    _, quarter, lanes = own_rows.shape
    for start, near, other in ((0, own, far), (quarter, own_core, far_core)):
        rows = slice(start, start + quarter)
        out[rows, 0:lanes] = (
            dot(own_rows[0], near[0:lanes, :]) + dot(far_rows[0], other[0:lanes, :])
        ).astype(out.dtype)
        out[rows, lanes:] = (
            dot(own_rows[1], near[lanes:, :], NT) + dot(far_rows[1], other[lanes:, :], NT)
        ).astype(out.dtype)


def sum_parts(parts, start, stop):
    total = parts[start].astype(F32)
    for peer in range(start + 1, stop):
        total = total + parts[peer].astype(F32)
    return total


def units_kernel(parts, out):
    total = sum_parts(parts, 0, parts.shape[0])
    units = total.shape[1] // 3
    gate_sum = total[:, 0:units]
    up_sum = total[:, units : 2 * units]
    hidden_grad = total[:, 2 * units :]
    sigmoid_gate = jax.nn.sigmoid(gate_sum)
    active = gate_sum * sigmoid_gate
    hidden = (active * up_sum).astype(out.dtype)
    gate_act = (
        hidden_grad * up_sum * sigmoid_gate * (1.0 + gate_sum * (1.0 - sigmoid_gate))
    ).astype(out.dtype)
    up_act = (hidden_grad * active).astype(out.dtype)
    for peer in range(out.shape[0]):
        out[peer, :, 0:units] = hidden
        out[peer, :, units : 2 * units] = gate_act
        out[peer, :, 2 * units :] = up_act


def apply_kernel(me, acts, own, far, own_core, far_core, out, result, stage):
    quarter = result.shape[0]
    lanes = own.shape[1]
    units = own.shape[0] - lanes
    peers = out.shape[0] // 2
    side = out.shape[-1]
    rows = quarter // peers
    near, other = slice(0, quarter), slice(quarter, 2 * quarter)
    for group, first, second in ((0, own, own_core), (1, far, far_core)):
        result[:, 0:lanes] = dot(acts[near, 0:units], first[lanes:, :]) + dot(
            acts[other, 0:units], second[lanes:, :]
        )
        result[:, lanes:] = dot(acts[near, units:], first[0:lanes, :], NT) + dot(
            acts[other, units:], second[0:lanes, :], NT
        )
        base = (me[0] if group == 0 else 1 - me[0]) * peers
        for peer in range(peers):
            for q in range(2 * lanes // side):
                stage[peer, q * rows : (q + 1) * rows, :] = result[
                    peer * rows : (peer + 1) * rows, q * side : (q + 1) * side
                ]
            out[base + peer] = stage[peer].astype(out.dtype)


def grads_kernel(acts, far_acts, own_rows, far_rows, own, sibling):
    _, quarter, lanes = own_rows.shape
    units = own.shape[0] - lanes
    for start, out in ((quarter, sibling), (0, own)):
        rows = slice(start, start + quarter)
        out[0:lanes, :] = (
            dot(own_rows[0], acts[rows, units:], TN) + dot(far_rows[0], far_acts[rows, units:], TN)
        ).astype(out.dtype)
        out[lanes:, :] = (
            dot(acts[rows, 0:units], own_rows[1], TN)
            + dot(far_acts[rows, 0:units], far_rows[1], TN)
        ).astype(out.dtype)


def finish_kernel(parts, output, input_grad):
    rows, lanes = output.shape
    part = rows // 2
    peers = parts.shape[0] // 2
    side = parts.shape[-1]
    chunks = lanes // side
    for group in range(2):
        total = sum_parts(parts, group * peers, (group + 1) * peers)
        for start, out in ((0, output), (chunks, input_grad)):
            for q in range(chunks):
                piece = total[(start + q) * part : (start + q + 1) * part]
                out[group * part : (group + 1) * part, q * side : (q + 1) * side] = piece.astype(
                    out.dtype
                )


def call(kernel, outs, args, smem=0, scratch=(), flops=0, limit=12 << 20):
    moved = sum(a.size * a.dtype.itemsize for a in args) + sum(
        o.size * jnp.dtype(o.dtype).itemsize for o in outs
    )
    single = len(outs) == 1
    return pl.pallas_call(
        kernel,
        out_shape=outs[0] if single else outs,
        in_specs=(SMEM,) * smem + (VMEM,) * (len(args) - smem),
        out_specs=VMEM if single else (VMEM,) * len(outs),
        scratch_shapes=scratch,
        compiler_params=pltpu.CompilerParams(vmem_limit_bytes=limit),
        cost_estimate=pl.CostEstimate(flops=flops, bytes_accessed=moved, transcendentals=0),
    )(*args)


def exchange(blocks, axis):
    return lax.all_to_all(blocks, axis, split_axis=0, concat_axis=0, tiled=True)


def swap(block, axis):
    return lax.ppermute(block, axis, [(0, 1), (1, 0)])


def body(tokens, cotangent, gate_tiles, up_tiles, down_tiles, tile_index, tile_counts):
    rows, lanes = tokens.shape
    slots, side, _ = gate_tiles.shape
    row_peers = lax.axis_size("xh") * lax.axis_size("yl")
    peers = lax.axis_size("yz")
    units = 2 * side
    quarter = peers * rows // 2
    share = 2 * quarter // row_peers
    packed = lanes // side * rows
    flops = 24 * quarter * lanes * units
    counts = tile_counts.reshape(3)
    index = tile_index.transpose(0, 2, 1)
    me = lax.axis_index("xl").astype(jnp.int32).reshape(1)
    shape = jax.ShapeDtypeStruct

    dense = (lanes + units, lanes)
    spread, own = call(
        start_kernel,
        (shape((2 * peers, packed, side), BF16), shape(dense, BF16)),
        (index, counts, tokens, cotangent, gate_tiles, up_tiles, down_tiles),
        smem=2,
        scratch=(pltpu.VMEM((2 * packed, side), F32),),
        limit=None,
    )
    blocks = exchange(spread, ("xl", "yz"))
    far = swap(own, "xl")
    own_core = swap(own, "core")
    far_core = swap(far, "core")
    weights = (own, far, own_core, far_core)
    own_rows, far_rows = call(
        unpack_kernel,
        (shape((2, quarter, lanes), BF16),) * 2,
        (me, blocks),
        smem=1,
        scratch=(pltpu.VMEM((2, quarter, 2 * lanes), F32),),
        flops=UNPACK,
    )
    parts = call(
        partial_kernel,
        (shape((2 * quarter, 3 * units), BF16),),
        (own_rows, far_rows, *weights),
        flops=flops,
    )
    parts = exchange(parts.reshape(row_peers, share, 3 * units), ("xh", "yl"))
    acts = call(units_kernel, (shape(parts.shape, BF16),), (parts,))
    acts = exchange(acts, ("xh", "yl")).reshape(2 * quarter, 3 * units)
    sums = call(
        apply_kernel,
        (shape((2 * peers, packed, side), BF16),),
        (me, acts, *weights),
        smem=1,
        scratch=(pltpu.VMEM((quarter, 2 * lanes), F32), pltpu.VMEM((peers, packed, side), F32)),
        flops=flops,
    )
    sums = exchange(sums, ("xl", "yz"))
    far_acts, far_rows = swap(acts, "xl"), swap(far_rows, "xl")
    own_grad, sibling_grad = call(
        grads_kernel,
        (shape(dense, F32), shape(dense, BF16)),
        (acts, far_acts, own_rows, far_rows),
        flops=flops,
    )
    gate_grad, up_grad, down_grad = call(
        tiles_kernel,
        (shape((slots, side, side), F32),) * 3,
        (index, counts, own_grad, swap(sibling_grad, "core")),
        smem=2,
    )
    output, input_grad = call(finish_kernel, (shape((rows, lanes), BF16),) * 2, (sums,), flops=LONG)
    return (output, input_grad, gate_grad, up_grad, down_grad)


def solution(mesh):
    row_size, col_size = mesh.shape["row"], mesh.shape["col"]
    split = Mesh(
        mesh.devices.reshape(row_size // 4, 2, 2, col_size // 2, 2),
        ("xh", "xl", "yl", "yz", "core"),
    )
    row, col = ("xh", "xl", "yl"), ("yz", "core")
    blocks = P(col, row)
    tiles = P(row, col, None)
    small = P(None, row, col)
    return jax.shard_map(
        body,
        mesh=split,
        in_specs=(blocks, blocks, tiles, tiles, tiles, small, small),
        out_specs=(blocks, blocks, tiles, tiles, tiles),
        check_vma=False,
    )
```
